512 devices in a mesh: level: 16 (over z_lo, x, core), band: 32 (over y, z_hi).
Axes of the slice: x: 4, y: 8, z: 8 (z_hi: 4, z_lo: 2; z = z_hi * 2 + z_lo), core: 2. Of those that a mesh axis runs over, the one named last changes fastest.
Arguments:
- features: bfloat16 [65536, 128], P('band'), may hold values from -6 to 6
- block_perm: int32 [16, 32, 8], P('level', 'band'), may hold values from 0 to 7, each once within a row
- tile_rows: int32 [16, 1152], P('level', 'band'), may hold values from 0 to 255, as said below
- tile_cols: int32 [16, 1152], P('level', 'band'), may hold values from 0 to 255, as said below
- tile_vals: bfloat16 [16, 1152, 256, 256], P('level', 'band'), may hold values from -0.1875 to 0.1875
Outputs:
- forward: bfloat16 [32, 2048, 128], P('band', 'level')
- backward: bfloat16 [32, 2048, 128], P('band', 'level')
The draws below stay inside these ranges and needn't reach their ends.
Inputs may be any that keep to these rules, and one draw needn't show every extreme that they name: `block_perm`: each band device's 8 entries of a level are a permutation of 0 to 7. `tile_rows`: the 36 tiles stored at band index b of a level each have either block row in b's blocks [b * 8, (b + 1) * 8) and block column in the blocks of band indices b - 1, b, b + 1 or below 2, or block row below 2 and block column in b's blocks; positions may repeat. `tile_cols`: as for tile_rows, paired entry by entry.
All inputs are finite; a program needn't handle non-finite values.
Results may differ from the reference program's by a relative error of at most 0.001.
Values may be sent and summed in bfloat16 or wider, within the bound.
A program may use at most 128 MiB of HBM per device.

```python
import jax
import jax.numpy as jnp

F = 128
TILE = 256
RDEV = 2048
K = 36
HEADB = 2
RB = 8
NBLK = 256
NROWS = 65536
N_LEVEL = 16
N_BAND = 32


def tile_layout(key):
    key = jax.random.fold_in(key, 7)
    keys = jax.random.split(key, 6)
    shape = (N_LEVEL, N_BAND * K)
    flat = jnp.arange(N_BAND * K, dtype=jnp.int32)
    band_of = jnp.broadcast_to(flat // K, shape)
    slot = jnp.broadcast_to(flat % K, shape)
    own_row = band_of * RB + jax.random.randint(keys[0], shape, 0, RB)
    own_col = band_of * RB + jax.random.randint(keys[1], shape, 0, RB)
    steps_near = jax.random.randint(keys[2], shape, -1, 2)
    near_band = jnp.clip(band_of + steps_near, 0, N_BAND - 1)
    near_col = near_band * RB + jax.random.randint(keys[3], shape, 0, RB)
    head_pick = jax.random.randint(keys[4], shape, 0, HEADB)
    row_head = slot < K // 6
    col_head = (slot >= K // 6) & (slot < K // 3)
    rows = jnp.where(row_head, head_pick, own_row)
    cols = jnp.where(row_head, own_col, jnp.where(col_head, head_pick, near_col))
    rows = jnp.where(slot == 0, 0, rows)
    last_row = band_of * RB + RB - 1
    last_col = jnp.minimum(band_of + 1, N_BAND - 1) * RB + RB - 1
    rows = jnp.where(slot == K - 1, last_row, rows)
    cols = jnp.where(slot == K - 1, last_col, cols)
    scores = jax.random.randint(keys[5], (N_LEVEL, N_BAND, K), 0, 1 << 20) * K + jnp.arange(K, dtype=jnp.int32)
    slot_order = jnp.argsort(scores, axis=-1, stable=True)
    rows = jnp.take_along_axis(rows.reshape(N_LEVEL, N_BAND, K), slot_order, axis=-1).reshape(shape)
    cols = jnp.take_along_axis(cols.reshape(N_LEVEL, N_BAND, K), slot_order, axis=-1).reshape(shape)
    return (rows.astype(jnp.int32), cols.astype(jnp.int32))


def draw_tile_rows(key, part):
    return tile_layout(key)[0]


def draw_tile_cols(key, part):
    return tile_layout(key)[1]


def level_of(own_key, extent, cuts, low, largest):
    level = 1.0
    for position, parts in cuts:
        heights = jax.random.uniform(jax.random.fold_in(jax.random.fold_in(own_key, 6), position), (parts,), jnp.float32, low / len(cuts), largest / len(cuts))
        level = level * jnp.repeat(jnp.exp(heights), extent[position] // parts).reshape((-1,) + (1,) * (len(extent) - 1 - position))
    return level


def scatter_about(rng, shape, scale, reach, cuts=(), held_as=jnp.bfloat16):
    level = level_of(rng, shape, cuts, -0.22, 0.18) if cuts else 1.0
    values = jax.random.normal(rng, shape, jnp.float32) * scale * level
    return jnp.minimum(jnp.maximum(values, -reach), reach).astype(held_as)


def setup_inputs(seed: int = 0) -> dict:
    arg_keys = jax.random.split(jax.random.key(seed), 6)
    return {
        "features": scatter_about(arg_keys[0], (NROWS, F), 1.0, 6.0, ((0, 32),)),
        "block_perm": jax.vmap(lambda own: jax.random.permutation(own, RB))(jax.random.split(arg_keys[1], N_LEVEL * N_BAND)).reshape((N_LEVEL, N_BAND, RB)).astype(jnp.int32),
        "tile_rows": draw_tile_rows(jax.random.fold_in(arg_keys[5], 71), 0),
        "tile_cols": draw_tile_cols(jax.random.fold_in(arg_keys[5], 71), 0),
        "tile_vals": scatter_about(arg_keys[4], (N_LEVEL, NBLK * K // RB, TILE, TILE), (TILE * K // RB) ** -0.5, 0.1875, ((0, 16), (1, 32))),
    }


def reference(features, block_perm, tile_rows, tile_cols, tile_vals):
    x_blocks = features.reshape(NBLK, TILE, F).astype(jnp.float32)
    fwd = jnp.zeros((NBLK, TILE, F), jnp.float32)
    bwd = jnp.zeros((NBLK, TILE, F), jnp.float32)
    for level_id in range(N_LEVEL):
        global_of = (jnp.arange(N_BAND, dtype=jnp.int32)[:, None] * RB + block_perm[level_id].astype(jnp.int32)).reshape(-1)
        level_x = x_blocks[global_of]
        rows = tile_rows[level_id].astype(jnp.int32)
        cols = tile_cols[level_id].astype(jnp.int32)
        vals = tile_vals[level_id].astype(jnp.float32)
        prod_fwd = jnp.einsum("kij,kjf->kif", vals, level_x[cols])
        prod_bwd = jnp.einsum("kij,kif->kjf", vals, level_x[rows])
        level_fwd = jax.ops.segment_sum(prod_fwd, rows, num_segments=NBLK)
        level_bwd = jax.ops.segment_sum(prod_bwd, cols, num_segments=NBLK)
        fwd = fwd.at[global_of].add(level_fwd)
        bwd = bwd.at[global_of].add(level_bwd)
    forward = fwd.reshape(N_BAND, RDEV, F).astype(jnp.bfloat16)
    backward = bwd.reshape(N_BAND, RDEV, F).astype(jnp.bfloat16)
    return forward, backward
```

```python
import jax
import jax.numpy as jnp
from jax import lax
from jax.experimental import pallas as pl
from jax.experimental.pallas import tpu as pltpu
from jax.sharding import PartitionSpec as P

MESH = pl.DeviceIdType.MESH
NX, NY, NZ = 4, 8, 4
LEVELS, BANDS = 16, 32
RB, HALF, F, TILE, K = 8, 128, 128, 256, 36
UNITS = 6
Z_FIRST = (True, False, True, False, True, False)


def place():
    level = lax.axis_index("level")
    band = lax.axis_index("band")
    return level, band, level // 8, (level // 2) % NX, level % 2, band // NZ, band % NZ


def dev(level, band):
    return {"level": level, "band": band}


def remote(src, dst, send, recv, to):
    return pltpu.make_async_remote_copy(
        src_ref=src, dst_ref=dst, send_sem=send, recv_sem=recv, device_id=to, device_id_type=MESH
    )


def greet(barrier, to):
    pl.semaphore_signal(barrier, inc=1, device_id=to, device_id_type=MESH)


def at_x(level, x):
    return (level // 8) * 8 + x * 2 + level % 2


def gather_kernel(feat, perm, xs, perms, own_sem, near_s, near_r, core_s, core_r, far_s, far_r,
                  p_s, p_r, h1_s, h1_r, h2_s, h2_r, q1_s, q1_r, q2_s, q2_r, hz_s, hz_r, hx_s, hx_r,
                  hc_s, hc_r):
    level, band, zl, x, c, y, zh = place()
    flip = lax.rem(level + 8, LEVELS)
    near_band = lax.rem(band + jnp.where(zl == 0, BANDS - 1, 1), BANDS)
    up = lax.rem(band + 1, BANDS)
    down = lax.rem(band + BANDS - 1, BANDS)
    near_dev = dev(flip, near_band)
    pair_dev = dev(flip, band)
    core_dev = dev(level + 1 - 2 * c, band)
    x_devs = [dev(at_x(level, lax.rem(x + d, NX)), band) for d in (1, 2, 3)]
    barrier = pltpu.get_barrier_semaphore()
    for to in (near_dev, pair_dev, core_dev, *x_devs, dev(level, up), dev(level, down)):
        greet(barrier, to)

    @pl.when(band == 0)
    def _():
        for d in range(1, NZ):
            greet(barrier, dev(level, d))

    @pl.when((y == 0) & (zh != 0))
    def _():
        greet(barrier, dev(level, 0))

    @pl.when(y == 0)
    def _():
        for d in range(1, NY):
            greet(barrier, dev(level, d * NZ + zh))

    @pl.when(y != 0)
    def _():
        greet(barrier, dev(level, zh))

    pl.semaphore_wait(
        barrier, 8 + jnp.where(y == 0, jnp.where(zh == 0, NZ - 1 + NY - 1, 1 + NY - 1), 1)
    )

    own = pltpu.make_async_copy(feat, xs.at[1], own_sem.at[0])
    own.start()
    own_p = pltpu.make_async_copy(perm, perms.at[1], own_sem.at[1])
    own_p.start()
    to_up = remote(perm, perms.at[0], p_s.at[0], p_r.at[0], dev(level, up))
    to_down = remote(perm, perms.at[2], p_s.at[1], p_r.at[1], dev(level, down))
    to_up.start()
    to_down.start()
    near = [
        remote(feat.at[c, i], xs.at[0, c, i], near_s.at[i], near_r.at[i], near_dev)
        for i in range(NX)
    ]

    @pl.when(band == 0)
    def _():
        piece = pltpu.make_async_copy(feat.at[zl, x, c], xs.at[3, zl, x, c], own_sem.at[2])
        piece.start()
        first = pltpu.make_async_copy(perm, perms.at[3], own_sem.at[3])
        first.start()
        for d in range(1, NZ):
            remote(feat.at[zl, x, c], xs.at[3, zl, x, c], h1_s.at[d - 1], h1_r.at[0], dev(level, d)).start()
            remote(perm, perms.at[3], q1_s.at[d - 1], q1_r.at[0], dev(level, d)).start()
        piece.wait()
        first.wait()

    for copy in near:
        copy.start()
    h1_in = remote(feat.at[zl, x, c], xs.at[3, zl, x, c], h1_s.at[0], h1_r.at[0], dev(level, 0))
    q1_in = remote(perm, perms.at[3], q1_s.at[0], q1_r.at[0], dev(level, 0))

    @pl.when((y == 0) & (zh != 0))
    def _():
        h1_in.wait_recv()
        q1_in.wait_recv()

    def fan(d):
        to = dev(level, d * NZ + zh)
        return (
            remote(xs.at[3, zl, x, c], xs.at[3, zl, x, c], h2_s.at[d - 1], h2_r.at[0], to),
            remote(perms.at[3], perms.at[3], q2_s.at[d - 1], q2_r.at[0], to),
        )

    @pl.when(y == 0)
    def _():
        for d in range(1, NY):
            for copy in fan(d):
                copy.start()

    far = [
        remote(xs.at[0, c, i], xs.at[2, c, i], far_s.at[i], far_r.at[i], pair_dev) for i in range(NX)
    ]
    core = [
        remote(xs.at[s, c, i], xs.at[s, c, i], core_s.at[j, i], core_r.at[j, i], core_dev)
        for j, s in enumerate((0, 2))
        for i in range(NX)
    ]
    core_in = [
        remote(xs.at[s, 1 - c, i], xs.at[s, 1 - c, i], core_s.at[j, i], core_r.at[j, i], core_dev)
        for j, s in enumerate((0, 2))
        for i in range(NX)
    ]
    for i in range(NX):
        near[i].wait_recv()
        far[i].start()
        core[i].start()

    @pl.when(y != 0)
    def _():
        for copy in fan(1):
            copy.wait_recv()

    h_pair = remote(xs.at[3, zl, x, c], xs.at[3, zl, x, c], hz_s, hz_r, pair_dev)
    h_pair.start()
    for i in range(NX):
        far[i].wait_recv()
        core[NX + i].start()
    remote(xs.at[3, 1 - zl, x, c], xs.at[3, 1 - zl, x, c], hz_s, hz_r, pair_dev).wait_recv()
    h_x = []
    for d in range(3):
        copy = remote(xs.at[3, :, x, c], xs.at[3, :, x, c], hx_s.at[d], hx_r.at[d], x_devs[d])
        copy.start()
        h_x.append(copy)
    for d in range(3):
        source = lax.rem(x + NX - 1 - d, NX)
        remote(xs.at[3, :, source, c], xs.at[3, :, source, c], hx_s.at[d], hx_r.at[d], x_devs[d]).wait_recv()
    h_core = remote(xs.at[3, :, :, c], xs.at[3, :, :, c], hc_s, hc_r, core_dev)
    h_core.start()
    own.wait()
    own_p.wait()
    to_up.wait()
    to_down.wait()
    for copy in core_in:
        copy.wait_recv()
    remote(xs.at[3, :, :, 1 - c], xs.at[3, :, :, 1 - c], hc_s, hc_r, core_dev).wait_recv()
    for copy in (*near, *far, *core, h_pair, *h_x, h_core):
        copy.wait_send()

    @pl.when(band == 0)
    def _():
        for d in range(1, NZ):
            remote(feat.at[zl, x, c], xs.at[3, zl, x, c], h1_s.at[d - 1], h1_r.at[0], dev(level, d)).wait_send()
            remote(perm, perms.at[3], q1_s.at[d - 1], q1_r.at[0], dev(level, d)).wait_send()

    @pl.when(y == 0)
    def _():
        for d in range(1, NY):
            for copy in fan(d):
                copy.wait_send()


def product_kernel(rows, cols, perms, xs, vals, sums, held, sems):
    level, band, zl, x, c, y, zh = place()
    groups = 6
    each = K // groups
    loads = [
        pltpu.make_async_copy(vals.at[pl.ds(g * each, each)], held.at[pl.ds(g * each, each)], sems.at[g])
        for g in range(groups)
    ]
    for load in loads:
        load.start()
    sums[...] = jnp.zeros_like(sums)
    low = (band - 1) * RB

    def tile_step(k, carry):
        row, col = rows[0, k], cols[0, k]
        own = (row >= band * RB) & (row < (band + 1) * RB)
        near = (col >= low) & (col < low + 3 * RB)
        r_slot = jnp.where(own, 1, 3)
        r_block = perms[r_slot, 0, jnp.where(own, row - band * RB, row)]
        rel = col - low
        side = jnp.where(near, rel // RB, 3)
        c_block = perms[side, 0, jnp.where(near, rel % RB, col)]
        x_slot = jnp.where(side == 1, 1, jnp.where(side == 3, 3, jnp.where((side == 0) == (zl == 0), 0, 2)))
        a = held[k]
        fwd = jnp.dot(a, xs[x_slot * RB + c_block], preferred_element_type=jnp.float32)
        f_out = jnp.where(own, 4, 0) * RB + r_block
        sums[f_out] += fwd
        bwd = lax.dot_general(
            a, xs[r_slot * RB + r_block], (((0,), (0,)), ((), ())), preferred_element_type=jnp.float32
        )
        b_win = jnp.where(side == 1, 5, jnp.where(side == 0, 2, jnp.where(side == 2, 3, 1)))
        b_out = b_win * RB + c_block
        sums[b_out] += bwd
        return carry

    for g in range(groups):
        loads[g].wait()
        lax.fori_loop(g * each, (g + 1) * each, tile_step, 0)


def reduce_kernel(w, fwd_out, bwd_out, rc, rz, xa, xb, acc, tot, ry, hs, rzh, rr, rl, rrt,
                  c_s, c_r, z_s, z_r, a_s, a_r, b_s, b_r, s_s, s_r, y_s, y_r, q_s, q_r, t_s, t_r):
    level, band, zl, x, c, y, zh = place()
    flip = lax.rem(level + 8, LEVELS)
    up = dev(level, lax.rem(band + 1, BANDS))
    down = dev(level, lax.rem(band + BANDS - 1, BANDS))
    pair_dev = dev(flip, band)
    core_dev = dev(level + 1 - 2 * c, band)
    xp, xm, xf = lax.rem(x + 1, NX), lax.rem(x + 3, NX), lax.rem(x + 2, NX)
    x_up, x_down = dev(at_x(level, xp), band), dev(at_x(level, xm), band)
    y_devs = [dev(level, lax.rem(y + d, NY) * NZ + zh) for d in range(1, NY)]
    barrier = pltpu.get_barrier_semaphore()
    for to in (pair_dev, core_dev, x_up, x_down, up, down, *y_devs):
        greet(barrier, to)

    @pl.when(zh == 0)
    def _():
        for d in range(1, NZ):
            greet(barrier, dev(level, band + d))

    @pl.when(zh != 0)
    def _():
        greet(barrier, dev(level, y * NZ))

    pl.semaphore_wait(barrier, 6 + NY - 1 + jnp.where(zh == 0, NZ - 1, 1))

    sent = []

    def send(*args):
        copy = remote(*args)
        copy.start()
        sent.append(copy)
        return copy

    core = [
        send(w.at[u, :, :, 1 - c], rc.at[u], c_s.at[u], c_r.at[u], core_dev) for u in range(UNITS)
    ]
    pending = {}

    def ring_start(u, piece, n):
        half = HALF // 2
        pending[u] = [
            send(piece(xf).at[:, pl.ds(0, half)], xa.at[u, 0, pl.ds(0, n)], a_s.at[u, 0], a_r.at[u, 0], x_up),
            send(piece(xf).at[:, pl.ds(half, half)], xa.at[u, 1, pl.ds(0, n)], a_s.at[u, 1], a_r.at[u, 1], x_down),
        ]

    def ring_pass(u, piece, n):
        half = HALF // 2
        for copy in pending[u]:
            copy.wait_recv()
        low = piece(xp).at[:, pl.ds(0, half)]
        low[...] += xa[u, 0, :n]
        high = piece(xm).at[:, pl.ds(half, half)]
        high[...] += xa[u, 1, :n]
        pending[u] = [
            send(piece(xp), xb.at[u, 0, pl.ds(0, n)], b_s.at[u, 0], b_r.at[u, 0], x_up),
            send(piece(xm), xb.at[u, 1, pl.ds(0, n)], b_s.at[u, 1], b_r.at[u, 1], x_down),
        ]

    def ring_end(u, piece, n):
        for copy in pending[u]:
            copy.wait_recv()
        return piece(x)[...] + xb[u, 0, :n] + xb[u, 1, :n]

    def z_piece(u):
        return lambda i: acc.at[u, pl.ds(i, 1)]

    def x_piece(u):
        return lambda i: rc.at[u, :, i]

    def step0(u):
        core[u].wait_recv()
        rc[u] += w[u, :, :, c]
        if Z_FIRST[u]:
            pending[u] = [send(rc.at[u, 1 - zl], rz.at[u], z_s.at[u], z_r.at[u], pair_dev)]
        else:
            ring_start(u, x_piece(u), 2)

    def step1(u):
        if Z_FIRST[u]:
            pending[u][0].wait_recv()
            acc[u] = rc[u, zl] + rz[u]
            ring_start(u, z_piece(u), 1)
        else:
            ring_pass(u, x_piece(u), 2)

    def step2(u):
        if Z_FIRST[u]:
            ring_pass(u, z_piece(u), 1)
        else:
            acc[u, pl.ds(0, 2)] = ring_end(u, x_piece(u), 2)
            pending[u] = [
                send(acc.at[u, pl.ds(1 - zl, 1)], rz.at[u, pl.ds(0, 1)], z_s.at[u], z_r.at[u], pair_dev)
            ]

    def step3(u):
        if Z_FIRST[u]:
            tot[u] = ring_end(u, z_piece(u), 1)[0].reshape(NY, HALF // NY, F)
        else:
            pending[u][0].wait_recv()
            tot[u] = (acc[u, zl] + rz[u, 0]).reshape(NY, HALF // NY, F)

    for u in range(UNITS):
        step0(u)
    for u in (0, 1):
        step1(u)
    for u in (0, 1):
        step2(u)
    for u in (2, 3):
        step1(u)
    for u in (0, 1):
        step3(u)
    y_in = []
    for d in range(1, NY):
        y_in.append(
            send(tot.at[pl.ds(0, 2), lax.rem(y + d, NY)], ry.at[d - 1], y_s.at[d - 1], y_r.at[d - 1], y_devs[d - 1])
        )
    for u in (2, 3):
        step2(u)
    for u in (4, 5):
        step1(u)
    for u in (2, 3):
        step3(u)
    side_r = send(tot.at[3], rl, s_s.at[0], s_r.at[0], up)
    side_l = send(tot.at[2], rrt, s_s.at[1], s_r.at[1], down)
    for copy in y_in:
        copy.wait_recv()
    hs[...] = tot[pl.ds(0, 2), y] + jnp.sum(ry[...], axis=0)

    def up_z():
        return remote(hs, rzh.at[zh - 1], q_s, q_r.at[zh - 1], dev(level, y * NZ))

    def to_root():
        return remote(hs, rr.at[y - 1], t_s, t_r.at[y - 1], dev(level, 0))

    @pl.when(zh != 0)
    def _():
        up_z().start()

    for u in (4, 5):
        step2(u)

    @pl.when(zh == 0)
    def _():
        for d in range(NZ - 1):
            remote(hs, rzh.at[d], q_s, q_r.at[d], dev(level, y * NZ + d + 1)).wait_recv()
        hs[...] += jnp.sum(rzh[...], axis=0)

    @pl.when((zh == 0) & (y != 0))
    def _():
        to_root().start()

    for u in (4, 5):
        step3(u)
    side_r.wait_recv()
    side_l.wait_recv()
    tot[5] += rl[...] + rrt[...]

    @pl.when(band == 0)
    def _():
        for d in range(NY - 1):
            remote(hs, rr.at[d], t_s, t_r.at[d], dev(level, (d + 1) * NZ)).wait_recv()
        for j in range(2):
            tot[4 + j, 0] += hs[j]
            for d in range(1, NY):
                tot[4 + j, d] += rr[d - 1, j]

    fwd_out[...] = tot[4].reshape(HALF, F).astype(jnp.bfloat16)
    bwd_out[...] = tot[5].reshape(HALF, F).astype(jnp.bfloat16)
    for copy in sent:
        copy.wait_send()

    @pl.when(zh != 0)
    def _():
        up_z().wait_send()

    @pl.when((zh == 0) & (y != 0))
    def _():
        to_root().wait_send()


def on_device(features, block_perm, tile_rows, tile_cols, tile_vals):
    vmem = pl.BlockSpec(memory_space=pltpu.VMEM)
    smem = pl.BlockSpec(memory_space=pltpu.SMEM)
    dma = pltpu.SemaphoreType.DMA
    perm = jnp.pad(block_perm[0], ((0, 7), (0, 128 - RB)))
    feat = features.reshape(2, NX, 2, HALF, F)
    xs, perms = pl.pallas_call(
        gather_kernel,
        out_shape=(
            jax.ShapeDtypeStruct((4, 2, NX, 2, HALF, F), jnp.bfloat16),
            jax.ShapeDtypeStruct((4, 8, 128), jnp.int32),
        ),
        in_specs=[vmem, vmem],
        out_specs=(vmem, vmem),
        scratch_shapes=[
            dma((4,)), dma((4,)), dma((4,)), dma((2, 4)), dma((2, 4)), dma((4,)), dma((4,)),
            dma((2,)), dma((2,)), dma((3,)), dma((1,)), dma((7,)), dma((1,)), dma((3,)), dma((1,)),
            dma((7,)), dma((1,)), dma(()), dma(()), dma((3,)), dma((3,)), dma(()), dma(()),
        ],
        compiler_params=pltpu.CompilerParams(collective_id=0, has_side_effects=True),
        name="gather",
    )(feat, perm)
    sums = pl.pallas_call(
        product_kernel,
        out_shape=jax.ShapeDtypeStruct((UNITS * RB, TILE, F), jnp.float32),
        in_specs=[smem, smem, smem, vmem, pl.BlockSpec(memory_space=pl.ANY)],
        out_specs=vmem,
        scratch_shapes=[pltpu.VMEM((K, TILE, TILE), jnp.bfloat16), dma((6,))],
        name="products",
    )(tile_rows, tile_cols, perms, xs.reshape(4 * RB, TILE, F), tile_vals[0])
    f32 = jnp.float32
    part = HALF // NY
    fwd, bwd = pl.pallas_call(
        reduce_kernel,
        out_shape=(jax.ShapeDtypeStruct((HALF, F), jnp.bfloat16),) * 2,
        in_specs=[vmem],
        out_specs=(vmem, vmem),
        scratch_shapes=[
            pltpu.VMEM((UNITS, 2, NX, HALF, F), f32),
            pltpu.VMEM((UNITS, NX, HALF, F), f32),
            pltpu.VMEM((UNITS, 2, 2, HALF // 2, F), f32),
            pltpu.VMEM((UNITS, 2, 2, HALF, F), f32),
            pltpu.VMEM((UNITS, NX, HALF, F), f32),
            pltpu.VMEM((UNITS, NY, part, F), f32),
            pltpu.VMEM((NY - 1, 2, part, F), f32),
            pltpu.VMEM((2, part, F), f32),
            pltpu.VMEM((NZ - 1, 2, part, F), f32),
            pltpu.VMEM((NY - 1, 2, part, F), f32),
            pltpu.VMEM((NY, part, F), f32),
            pltpu.VMEM((NY, part, F), f32),
            dma((6,)), dma((6,)), dma((6,)), dma((6,)), dma((6, 2)), dma((6, 2)), dma((6, 2)), dma((6, 2)),
            dma((2,)), dma((2,)), dma((7,)), dma((7,)), dma(()), dma((3,)), dma(()), dma((7,)),
        ],
        compiler_params=pltpu.CompilerParams(collective_id=1, has_side_effects=True),
        name="reduce",
    )(sums.reshape(UNITS, 2, NX, 2, HALF, F))
    return fwd[None], bwd[None]


def solution(mesh):
    return jax.shard_map(
        on_device,
        mesh=mesh,
        in_specs=(
            P("band", None),
            P("level", "band", None),
            P("level", "band"),
            P("level", "band"),
            P("level", "band", None, None),
        ),
        out_specs=(P("band", "level", None), P("band", "level", None)),
        check_vma=False,
    )
```
